32 devices in a mesh: seq: 2 (over core), fsdp: 16 (over z, y, x).
Axes of the slice: x: 2, y: 2, z: 4, core: 2. Of those that a mesh axis runs over, the one named last changes fastest.
Arguments:
- inputs: bfloat16 [2, 16, 512, 768], P(None, 'fsdp', 'seq'), may hold values from -6 to 6
- order: int32 [2, 16, 512], P(None, 'fsdp'), may hold values from 0 to 511, each once within a row
- lengths: int32 [2, 16, 2], P(None, 'fsdp'), may hold values from 128 to 384, as said below
- cotangent: bfloat16 [2, 16, 512, 768], P(None, 'fsdp', 'seq'), may hold values from -6 to 6
- weight_qkv: bfloat16 [768, 2304], P(('seq', 'fsdp')), may hold values from -0.21875 to 0.21875
- bias_qv: bfloat16 [1536], P(('seq', 'fsdp')), may hold values from -3 to 3
- weight_out: bfloat16 [768, 768], P(('seq', 'fsdp')), may hold values from -0.625 to 0.625
- bias_out: bfloat16 [768], P(('seq', 'fsdp')), may hold values from -3 to 3
- weight_in: bfloat16 [768, 3072], P(('seq', 'fsdp')), may hold values from -0.21875 to 0.21875
- bias_in: bfloat16 [3072], P(('seq', 'fsdp')), may hold values from -3 to 3
- weight_back: bfloat16 [3072, 768], P(('seq', 'fsdp')), may hold values from -0.21875 to 0.21875
- bias_back: bfloat16 [768], P(('seq', 'fsdp')), may hold values from -3 to 3
- gain_first: bfloat16 [768], P(('seq', 'fsdp')), may hold values from 0.25 to 1.75
- shift_first: bfloat16 [768], P(('seq', 'fsdp')), may hold values from -2 to 2
- gain_second: bfloat16 [768], P(('seq', 'fsdp')), may hold values from 0.25 to 1.75
- shift_second: bfloat16 [768], P(('seq', 'fsdp')), may hold values from -2 to 2
Outputs:
- block_out: bfloat16 [2, 16, 512, 768], P(None, 'fsdp', 'seq')
- input_grad: bfloat16 [2, 16, 512, 768], P(None, 'fsdp', 'seq')
- grad_weight_qkv: float32 [768, 2304], P(('seq', 'fsdp'))
- grad_bias_qv: float32 [1536], P(('seq', 'fsdp'))
- grad_weight_out: float32 [768, 768], P(('seq', 'fsdp'))
- grad_bias_out: float32 [768], P(('seq', 'fsdp'))
- grad_weight_in: float32 [768, 3072], P(('seq', 'fsdp'))
- grad_bias_in: float32 [3072], P(('seq', 'fsdp'))
- grad_weight_back: float32 [3072, 768], P(('seq', 'fsdp'))
- grad_bias_back: float32 [768], P(('seq', 'fsdp'))
- grad_gain_first: float32 [768], P(('seq', 'fsdp'))
- grad_shift_first: float32 [768], P(('seq', 'fsdp'))
- grad_gain_second: float32 [768], P(('seq', 'fsdp'))
- grad_shift_second: float32 [768], P(('seq', 'fsdp'))
The draws below stay inside these ranges and needn't reach their ends.
Inputs may be any that keep to these rules, and one draw needn't show every extreme that they name: Each row order[m, g, :] holds every packed position 0 to 511 once. Each row lengths[m, g, :] holds the lengths 512 * 3 // 4 and 128 of two sequences packed one after another, in either order.
All inputs are finite; a program needn't handle non-finite values.
Results may differ from the reference program's by a relative error of at most 0.014.
Values may be sent and summed in bfloat16 or wider, within the bound.
No kernel may reach another device: no remote copies, remote signals or barrier semaphores. Data moves between devices by JAX's collectives and lax.ppermute only.
A program may use at most 192 MiB of HBM per device.

```python
import jax
import jax.numpy as jnp
from jax import lax

D = 768
HEADS = 12
HD = 64
FF = 3072
MB = 2
NSEQ = 2
GROUP_TOK = 512
GROUPS = 16


def draw_lengths(key, part):
    flips = jax.random.randint(jax.random.fold_in(key, 7), (MB, GROUPS, 1), 0, 2).astype(jnp.int32)
    longer = GROUP_TOK * 3 // 4
    shorter = GROUP_TOK - longer
    first = jnp.where(flips == 1, longer, shorter).astype(jnp.int32)
    second = (GROUP_TOK - first).astype(jnp.int32)
    return jnp.concatenate([first, second], axis=2).astype(jnp.int32)


def spiked(array, rng, source, target, shards_of, factor):
    def block_of(dim):
        return (jnp.arange(array.shape[dim]) // (array.shape[dim] // shards_of)).reshape((-1,) + (1,) * (array.ndim - 1 - dim))

    one_side = jax.random.permutation(rng, shards_of)[block_of(target)]
    second = (block_of(target) + shards_of // 2) % shards_of
    return jnp.where((block_of(source) == one_side) | (block_of(source) == second), factor * array, array)


def block_scale(key, extent, pieces, least, largest):
    factor_of = 1.0
    for position, shards_of in pieces:
        steps = jax.random.uniform(jax.random.fold_in(jax.random.fold_in(key, 6), position), (shards_of,), jnp.float32, least / len(pieces), largest / len(pieces))
        factor_of = factor_of * jnp.repeat(jnp.exp(steps), extent[position] // shards_of).reshape((-1,) + (1,) * (len(extent) - 1 - position))
    return factor_of


def noise(key, dims, spread, limit, split=(), kind=jnp.bfloat16):
    array = jax.random.normal(key, dims, jnp.float32) * spread
    if len(split) > 0:
        array = block_scale(key, dims, split, -0.22, 0.18) * array
    return jnp.clip(array, min=-limit, max=limit).astype(kind)


def noise_with(own_key, dims, width, reach, pieces, heavy, held_as=jnp.bfloat16):
    drawn = width * jax.random.normal(own_key, dims, jnp.float32)
    if pieces:
        drawn = drawn * block_scale(own_key, dims, pieces, -0.22, 0.18)
    return jnp.clip(spiked(drawn, jax.random.fold_in(own_key, 3), *heavy), -reach, reach).astype(held_as)


def setup_inputs(seed: int = 0) -> dict:
    keys = jax.random.split(jax.random.key(seed), 17)
    inputs = noise(keys[0], (MB, GROUPS, GROUP_TOK, D), 1.0, 6.0, ((1, 16), (2, 2)))
    order = jax.vmap(lambda own: jax.random.permutation(own, GROUP_TOK))(jax.random.split(keys[1], MB * GROUPS)).reshape((MB, GROUPS, GROUP_TOK)).astype(jnp.int32)
    lengths = draw_lengths(jax.random.fold_in(keys[16], 71), 0)
    cotangent = noise_with(keys[3], (MB, GROUPS, GROUP_TOK, D), 1.0, 6.0, ((1, 16), (2, 2)), (1, 3, 16, 2.0))
    weight_qkv = noise(keys[4], (D, 3 * D), D ** -0.5, 0.21875, ((0, 32),))
    bias_qv = noise(keys[5], (2 * D,), 0.5, 3.0, ((0, 32),))
    weight_out = noise(keys[6], (D, D), (D // 8) ** -0.5, 0.625, ((0, 32),))
    bias_out = noise(keys[7], (D,), 0.5, 3.0, ((0, 32),))
    weight_in = noise(keys[8], (D, FF), D ** -0.5, 0.21875, ((0, 32),))
    bias_in = noise(keys[9], (FF,), 0.5, 3.0, ((0, 32),))
    weight_back = noise(keys[10], (FF, D), (FF // 4) ** -0.5, 0.21875, ((0, 32),))
    bias_back = noise(keys[11], (D,), 0.5, 3.0, ((0, 32),))
    gain_first = jnp.clip(1.0 + 0.15 * jax.random.normal(keys[12], (D,), jnp.float32), 0.25, 1.75).astype(jnp.bfloat16)
    shift_first = noise(keys[13], (D,), 0.3, 2.0, ((0, 32),))
    gain_second = jnp.clip(1.0 + 0.15 * jax.random.normal(keys[14], (D,), jnp.float32), 0.25, 1.75).astype(jnp.bfloat16)
    shift_second = noise(keys[15], (D,), 0.3, 2.0, ((0, 32),))
    return {"inputs": inputs, "order": order, "lengths": lengths, "cotangent": cotangent, "weight_qkv": weight_qkv, "bias_qv": bias_qv, "weight_out": weight_out, "bias_out": bias_out, "weight_in": weight_in, "bias_in": bias_in, "weight_back": weight_back, "bias_back": bias_back, "gain_first": gain_first, "shift_first": shift_first, "gain_second": gain_second, "shift_second": shift_second}


@jax.custom_vjp
def low(v):
    return lax.optimization_barrier(v.astype(jnp.bfloat16)).astype(jnp.float32)

@jax.custom_vjp
def low_back(v):
    return v

def low_keep(v):
    return (low(v), None)

def low_pass(kept, grad):
    return (grad,)

def back_keep(v):
    return (v, None)

def back_low(kept, grad):
    return (low(grad),)
low.defvjp(low_keep, low_pass)
low_back.defvjp(back_keep, back_low)
eps = 1e-05
score_scale = 0.125

def matmul_high(left, right):
    return jnp.dot(left, right, precision=lax.Precision.HIGHEST)

def layer_norm(values, gain, shift):
    row_mean = lax.optimization_barrier(jnp.mean(values, axis=-1, keepdims=True))
    centred = values - row_mean
    variance = lax.optimization_barrier(jnp.mean(centred * centred, axis=-1, keepdims=True))
    return centred * lax.rsqrt(variance + eps) * gain + shift

def gelu_tanh(values):
    return 0.5 * values * (1.0 + jnp.tanh(0.7978845608028654 * (values + 0.044715 * values * values * values)))

def attention(queries, key_rows, value_rows, slot_ids, seq_starts):
    block_rows = min(512, GROUP_TOK)
    block_count = GROUP_TOK // block_rows
    key_heads = key_rows.reshape(GROUP_TOK, HEADS, HD)
    value_heads = value_rows.reshape(GROUP_TOK, HEADS, HD)

    def one_block(block_id):
        first = (block_id * block_rows).astype(jnp.int32)
        q_blk = lax.dynamic_slice_in_dim(queries, first, block_rows, 0).reshape(block_rows, HEADS, HD)
        q_pos = lax.dynamic_slice_in_dim(slot_ids, first, block_rows, 0)
        q_start = lax.dynamic_slice_in_dim(seq_starts, first, block_rows, 0)
        raw_scores = jnp.einsum('qhd,khd->hqk', q_blk, key_heads, precision=lax.Precision.HIGHEST) * score_scale
        allowed = (slot_ids[None, :] <= q_pos[:, None]) & (slot_ids[None, :] >= q_start[:, None])
        scores = low_back(jnp.where(allowed[None], raw_scores, -1e+30))
        row_max = lax.optimization_barrier(jnp.max(scores, axis=-1, keepdims=True))
        expo = jnp.exp(scores - row_max)
        prob_rows = expo / lax.optimization_barrier(jnp.sum(expo, axis=-1, keepdims=True))
        head_out = jnp.einsum('hqk,khd->qhd', low(prob_rows), value_heads, precision=lax.Precision.HIGHEST)
        return head_out.reshape(block_rows, D)
    blocks = lax.map(jax.checkpoint(one_block), jnp.arange(block_count, dtype=jnp.int32))
    return blocks.reshape(GROUP_TOK, D)

def block_forward(params, inputs, slot_ids, seq_starts):
    weight_qkv, bias_qv, weight_out, bias_out, weight_in, bias_in, weight_back, bias_back, gain_first, shift_first, gain_second, shift_second = params
    normed = low(layer_norm(inputs, gain_first, shift_first))
    projected = matmul_high(normed, weight_qkv)
    queries = low_back(low(projected[:, :D] + bias_qv[:D]))
    key_rows = low_back(low(projected[:, D:2 * D]))
    value_rows = low_back(low(projected[:, 2 * D:] + bias_qv[D:]))
    attn_heads = attention(queries, key_rows, value_rows, slot_ids, seq_starts)
    attn_heads = low_back(low(attn_heads))
    mid_stream = inputs + low_back(matmul_high(attn_heads, weight_out)) + bias_out
    normed_two = low(layer_norm(mid_stream, gain_second, shift_second))
    pre_act = low_back(matmul_high(normed_two, weight_in) + bias_in)
    hidden = low(gelu_tanh(pre_act))
    return mid_stream + matmul_high(hidden, weight_back) + bias_back

def reference(inputs, order, lengths, cotangent, weight_qkv, bias_qv, weight_out, bias_out, weight_in, bias_in, weight_back, bias_back, gain_first, shift_first, gain_second, shift_second):
    params = tuple((p.astype(jnp.float32) for p in (weight_qkv, bias_qv, weight_out, bias_out, weight_in, bias_in, weight_back, bias_back, gain_first, shift_first, gain_second, shift_second)))
    streams = MB * GROUPS
    flat_inputs = inputs.reshape(streams, GROUP_TOK, D)
    flat_order = order.reshape(streams, GROUP_TOK).astype(jnp.int32)
    flat_lengths = lengths.reshape(streams, NSEQ).astype(jnp.int32)
    flat_cot = cotangent.reshape(streams, GROUP_TOK, D)

    def group_step(totals, group_item):
        x_grp, slot_ids, seq_lens, grad_rows = group_item
        seq_ends = jnp.cumsum(seq_lens).astype(jnp.int32)
        seq_starts = lax.optimization_barrier(jnp.max(jnp.where(seq_ends[None, :] <= slot_ids[:, None], seq_ends[None, :], 0), axis=1)).astype(jnp.int32)

        def forward(weights, block_in):
            return block_forward(weights, block_in, slot_ids, seq_starts)
        outputs, pull = jax.vjp(forward, params, x_grp.astype(jnp.float32))
        gradients, grad_in = pull(grad_rows.astype(jnp.float32))
        totals = jax.tree.map(lambda a, b: a + b, totals, gradients)
        return (totals, (outputs.astype(jnp.bfloat16), grad_in.astype(jnp.bfloat16)))
    start_totals = jax.tree.map(jnp.zeros_like, params)
    totals, (outputs, grad_ins) = lax.scan(group_step, start_totals, (flat_inputs, flat_order, flat_lengths, flat_cot))
    block_out = outputs.reshape(MB, GROUPS, GROUP_TOK, D)
    input_grad = grad_ins.reshape(MB, GROUPS, GROUP_TOK, D)
    return (block_out, input_grad, totals[0], totals[1], totals[2], totals[3], totals[4], totals[5], totals[6], totals[7], totals[8], totals[9], totals[10], totals[11])
```

```python
import jax
import jax.numpy as jnp
from jax import lax
from jax.experimental import pallas as pl
from jax.experimental.pallas import tpu as pltpu
from jax.sharding import PartitionSpec as P

D = 768
HEADS = 12
HD = 64
MB = 2


eps = 1e-05
score_scale = 0.125


def norm_parts(values):
    row_mean = jnp.mean(values, axis=-1, keepdims=True)
    centred = values - row_mean
    inv_std = lax.rsqrt(jnp.mean(centred * centred, axis=-1, keepdims=True) + eps)
    return (centred * inv_std, inv_std)


def norm_back(grad_norm, x_hat, inv_std, gain):
    scaled = grad_norm * gain
    return inv_std * (
        scaled
        - jnp.mean(scaled, axis=-1, keepdims=True)
        - x_hat * jnp.mean(scaled * x_hat, axis=-1, keepdims=True)
    )


def gelu_tanh(values):
    return (
        0.5
        * values
        * (1.0 + jnp.tanh(0.7978845608028654 * (values + 0.044715 * values * values * values)))
    )


def dot_first(left, right):
    return lax.dot_general(
        left, right, (((0,), (0,)), ((), ())), preferred_element_type=jnp.float32
    )


def dot_last(left, right):
    return lax.dot_general(
        left, right, (((1,), (1,)), ((), ())), preferred_element_type=jnp.float32
    )


def head_scores(queries, key_rows, head_id, allowed):
    q_head = lax.dynamic_slice_in_dim(queries, head_id * HD, HD, 1)
    k_head = lax.dynamic_slice_in_dim(key_rows, head_id * HD, HD, 1)
    raw_scores = dot_last(q_head, k_head) * score_scale
    return (jnp.where(allowed, raw_scores, -1e30), q_head, k_head)


def attend(queries, key_rows, value_rows, allowed):
    rows_here = queries.shape[0]

    def one_head(head_id, carry):
        attn_out, log_sums = carry
        scores, q_head, k_head = head_scores(queries, key_rows, head_id, allowed)
        row_max = jnp.max(scores, axis=1, keepdims=True)
        expo = jnp.exp(scores - row_max)
        row_sum = jnp.sum(expo, axis=1, keepdims=True)
        prob_rows = (expo / row_sum).astype(jnp.bfloat16)
        v_head = lax.dynamic_slice_in_dim(value_rows, head_id * HD, HD, 1)
        head_out = jnp.dot(prob_rows, v_head, preferred_element_type=jnp.float32)
        attn_out = lax.dynamic_update_slice_in_dim(attn_out, head_out, head_id * HD, 1)
        log_sums = lax.dynamic_update_slice_in_dim(log_sums, row_max + jnp.log(row_sum), head_id, 1)
        return (attn_out, log_sums)

    start = (jnp.zeros((rows_here, D), jnp.float32), jnp.zeros((rows_here, HEADS), jnp.float32))
    return lax.fori_loop(0, HEADS, one_head, start)


def attend_back(queries, key_rows, value_rows, allowed, log_sums, d_heads):
    rows_here = queries.shape[0]
    key_count = key_rows.shape[0]

    def one_head(head_id, carry):
        d_query, d_keys, d_values = carry
        scores, q_head, k_head = head_scores(queries, key_rows, head_id, allowed)
        head_lse = lax.dynamic_slice_in_dim(log_sums, head_id, 1, 1)
        prob_rows = jnp.exp(scores - head_lse)
        v_head = lax.dynamic_slice_in_dim(value_rows, head_id * HD, HD, 1)
        dh_head = lax.dynamic_slice_in_dim(d_heads, head_id * HD, HD, 1)
        d_prob = dot_last(dh_head, v_head)
        centre = jnp.sum(prob_rows * d_prob, axis=1, keepdims=True)
        d_scores = (prob_rows * (d_prob - centre)).astype(jnp.bfloat16)
        dq_head = score_scale * jnp.dot(d_scores, k_head, preferred_element_type=jnp.float32)
        dk_head = score_scale * dot_first(d_scores, q_head)
        dv_head = dot_first(prob_rows.astype(jnp.bfloat16), dh_head)
        d_query = lax.dynamic_update_slice_in_dim(d_query, dq_head, head_id * HD, 1)
        d_keys = lax.dynamic_update_slice_in_dim(d_keys, dk_head, head_id * HD, 1)
        d_values = lax.dynamic_update_slice_in_dim(d_values, dv_head, head_id * HD, 1)
        return (d_query, d_keys, d_values)

    start = (
        jnp.zeros((rows_here, D), jnp.float32),
        jnp.zeros((key_count, D), jnp.float32),
        jnp.zeros((key_count, D), jnp.float32),
    )
    return lax.fori_loop(0, HEADS, one_head, start)


def local(
    inputs,
    order,
    lengths,
    cotangent,
    weight_qkv,
    bias_qv,
    weight_out,
    bias_out,
    weight_in,
    bias_in,
    weight_back,
    bias_back,
    gain_first,
    shift_first,
    gain_second,
    shift_second,
):
    seq_pos = lax.axis_index("seq")
    rows_here = inputs.shape[2]
    totals = None
    outputs = []
    in_grads = []
    for micro in range(MB):
        x_rows = inputs[micro, 0]
        x_float = x_rows.astype(jnp.float32)
        slot_ids = order[micro, 0]
        my_slots = lax.dynamic_slice_in_dim(slot_ids, seq_pos * rows_here, rows_here, 0)
        seq_ends = jnp.cumsum(lengths[micro, 0])
        all_starts = jnp.max(
            jnp.where(seq_ends[None, :] <= slot_ids[:, None], seq_ends[None, :], 0), axis=1
        )
        seq_starts = lax.dynamic_slice_in_dim(all_starts, seq_pos * rows_here, rows_here, 0)
        allowed = (slot_ids[None, :] <= my_slots[:, None]) & (
            slot_ids[None, :] >= seq_starts[:, None]
        )
        gathered = (
            lax.all_gather(weight_qkv, ("seq", "fsdp"), axis=0, tiled=True),
            lax.all_gather(bias_qv, ("seq", "fsdp"), axis=0, tiled=True),
            lax.all_gather(weight_out, ("seq", "fsdp"), axis=0, tiled=True),
            lax.all_gather(bias_out, ("seq", "fsdp"), axis=0, tiled=True),
            lax.all_gather(weight_in, ("seq", "fsdp"), axis=0, tiled=True),
            lax.all_gather(bias_in, ("seq", "fsdp"), axis=0, tiled=True),
            lax.all_gather(weight_back, ("seq", "fsdp"), axis=0, tiled=True),
            lax.all_gather(bias_back, ("seq", "fsdp"), axis=0, tiled=True),
            lax.all_gather(gain_first, ("seq", "fsdp"), axis=0, tiled=True),
            lax.all_gather(shift_first, ("seq", "fsdp"), axis=0, tiled=True),
            lax.all_gather(gain_second, ("seq", "fsdp"), axis=0, tiled=True),
            lax.all_gather(shift_second, ("seq", "fsdp"), axis=0, tiled=True),
        )
        (
            qkv_mat,
            qv_vec,
            out_mat,
            out_vec,
            in_mat,
            in_vec,
            back_mat,
            back_vec,
            gain_one,
            shift_one,
            gain_two,
            shift_two,
        ) = gathered
        x_hat_one, inv_one = norm_parts(x_float)
        normed = (x_hat_one * gain_one + shift_one).astype(jnp.bfloat16)
        projected = jnp.dot(normed, qkv_mat, preferred_element_type=jnp.float32)
        queries = (projected[:, :D] + qv_vec[:D]).astype(jnp.bfloat16)
        key_rows = projected[:, D : 2 * D].astype(jnp.bfloat16)
        value_rows = (projected[:, 2 * D :] + qv_vec[D:]).astype(jnp.bfloat16)
        all_keys, all_values = (
            lax.all_gather(key_rows, "seq", axis=0, tiled=True),
            lax.all_gather(value_rows, "seq", axis=0, tiled=True),
        )
        attn_float, log_sums = attend(queries, all_keys, all_values, allowed)
        attn_heads = attn_float.astype(jnp.bfloat16)
        mid_stream = (
            x_float + jnp.dot(attn_heads, out_mat, preferred_element_type=jnp.float32) + out_vec
        )
        x_hat_two, inv_two = norm_parts(mid_stream)
        normed_two = (x_hat_two * gain_two + shift_two).astype(jnp.bfloat16)
        pre_act = jnp.dot(normed_two, in_mat, preferred_element_type=jnp.float32) + in_vec
        hidden_float, gelu_pull = jax.vjp(gelu_tanh, pre_act)
        hidden = hidden_float.astype(jnp.bfloat16)
        result = (
            mid_stream + jnp.dot(hidden, back_mat, preferred_element_type=jnp.float32) + back_vec
        )
        outputs.append(result.astype(jnp.bfloat16))
        gathered = (
            lax.all_gather(weight_qkv, ("seq", "fsdp"), axis=0, tiled=True),
            lax.all_gather(bias_qv, ("seq", "fsdp"), axis=0, tiled=True),
            lax.all_gather(weight_out, ("seq", "fsdp"), axis=0, tiled=True),
            lax.all_gather(bias_out, ("seq", "fsdp"), axis=0, tiled=True),
            lax.all_gather(weight_in, ("seq", "fsdp"), axis=0, tiled=True),
            lax.all_gather(bias_in, ("seq", "fsdp"), axis=0, tiled=True),
            lax.all_gather(weight_back, ("seq", "fsdp"), axis=0, tiled=True),
            lax.all_gather(bias_back, ("seq", "fsdp"), axis=0, tiled=True),
            lax.all_gather(gain_first, ("seq", "fsdp"), axis=0, tiled=True),
            lax.all_gather(shift_first, ("seq", "fsdp"), axis=0, tiled=True),
            lax.all_gather(gain_second, ("seq", "fsdp"), axis=0, tiled=True),
            lax.all_gather(shift_second, ("seq", "fsdp"), axis=0, tiled=True),
        )
        (
            qkv_mat,
            qv_vec,
            out_mat,
            out_vec,
            in_mat,
            in_vec,
            back_mat,
            back_vec,
            gain_one,
            shift_one,
            gain_two,
            shift_two,
        ) = gathered
        grad_rows = cotangent[micro, 0]
        grad_float = grad_rows.astype(jnp.float32)
        d_back_mat = dot_first(hidden, grad_rows)
        d_back_vec = jnp.sum(grad_float, axis=0)
        d_hidden = dot_last(grad_rows, back_mat)
        d_pre = gelu_pull(d_hidden)[0].astype(jnp.bfloat16)
        d_in_mat = dot_first(normed_two, d_pre)
        d_in_vec = jnp.sum(d_pre.astype(jnp.float32), axis=0)
        d_norm_two = dot_last(d_pre, in_mat)
        d_gain_two = jnp.sum(d_norm_two * x_hat_two, axis=0)
        d_shift_two = jnp.sum(d_norm_two, axis=0)
        d_mid = grad_float + norm_back(d_norm_two, x_hat_two, inv_two, gain_two)
        d_out_vec = jnp.sum(d_mid, axis=0)
        d_mid_low = d_mid.astype(jnp.bfloat16)
        d_out_mat = dot_first(attn_heads, d_mid_low)
        d_heads = dot_last(d_mid_low, out_mat).astype(jnp.bfloat16)
        d_query, d_keys_all, d_values_all = attend_back(
            queries, all_keys, all_values, allowed, log_sums, d_heads
        )
        d_keys, d_values = (
            lax.psum_scatter(
                d_keys_all.astype(jnp.bfloat16), "seq", scatter_dimension=0, tiled=True
            ).astype(jnp.float32),
            lax.psum_scatter(
                d_values_all.astype(jnp.bfloat16), "seq", scatter_dimension=0, tiled=True
            ).astype(jnp.float32),
        )
        d_mixed = jnp.concatenate([d_query, d_keys, d_values], axis=1).astype(jnp.bfloat16)
        d_qkv_mat = dot_first(normed, d_mixed)
        column_sums = jnp.sum(d_mixed.astype(jnp.float32), axis=0)
        d_qv_vec = jnp.concatenate([column_sums[:D], column_sums[2 * D :]], axis=0)
        d_norm_one = dot_last(d_mixed, qkv_mat)
        d_gain_one = jnp.sum(d_norm_one * x_hat_one, axis=0)
        d_shift_one = jnp.sum(d_norm_one, axis=0)
        d_inputs = d_mid + norm_back(d_norm_one, x_hat_one, inv_one, gain_one)
        in_grads.append(d_inputs.astype(jnp.bfloat16))
        gradients = (
            d_qkv_mat,
            d_qv_vec,
            d_out_mat,
            d_out_vec,
            d_in_mat,
            d_in_vec,
            d_back_mat,
            d_back_vec,
            d_gain_one,
            d_shift_one,
            d_gain_two,
            d_shift_two,
        )
        if totals is None:
            totals = tuple(gradients)
        else:
            totals = tuple((a + b for a, b in zip(totals, gradients)))
    totals = (
        lax.psum_scatter(totals[0], ("seq", "fsdp"), scatter_dimension=0, tiled=True),
        lax.psum_scatter(totals[1], ("seq", "fsdp"), scatter_dimension=0, tiled=True),
        lax.psum_scatter(totals[2], ("seq", "fsdp"), scatter_dimension=0, tiled=True),
        lax.psum_scatter(totals[3], ("seq", "fsdp"), scatter_dimension=0, tiled=True),
        lax.psum_scatter(totals[4], ("seq", "fsdp"), scatter_dimension=0, tiled=True),
        lax.psum_scatter(totals[5], ("seq", "fsdp"), scatter_dimension=0, tiled=True),
        lax.psum_scatter(totals[6], ("seq", "fsdp"), scatter_dimension=0, tiled=True),
        lax.psum_scatter(totals[7], ("seq", "fsdp"), scatter_dimension=0, tiled=True),
        lax.psum_scatter(totals[8], ("seq", "fsdp"), scatter_dimension=0, tiled=True),
        lax.psum_scatter(totals[9], ("seq", "fsdp"), scatter_dimension=0, tiled=True),
        lax.psum_scatter(totals[10], ("seq", "fsdp"), scatter_dimension=0, tiled=True),
        lax.psum_scatter(totals[11], ("seq", "fsdp"), scatter_dimension=0, tiled=True),
    )
    block_out = jnp.stack(outputs)[:, None]
    input_grad = jnp.stack(in_grads)[:, None]
    return (
        block_out,
        input_grad,
        totals[0],
        totals[1],
        totals[2],
        totals[3],
        totals[4],
        totals[5],
        totals[6],
        totals[7],
        totals[8],
        totals[9],
        totals[10],
        totals[11],
    )


BLK = 128


def row_ranges(rows):
    longer = rows * 3 // 4
    ranges, offset = [], 0
    for first in range(0, rows, BLK):
        begin = 0 if first < longer else longer
        width = first + BLK - begin
        ranges.append((first, begin, width, offset))
        offset += width
    return ranges, offset


def attend_kernel(rows, q_ref, k_ref, v_ref, out_ref, prob_ref):
    low_half = lax.broadcasted_iota(jnp.int32, (BLK, 2 * HD), 1) < HD
    tri = lax.broadcasted_iota(jnp.int32, (BLK, BLK), 1) <= lax.broadcasted_iota(
        jnp.int32, (BLK, BLK), 0
    )
    ranges, _ = row_ranges(rows)
    for first, begin, width, offset in ranges:
        q_blk = q_ref[first : first + BLK, :]
        keys = k_ref[begin : begin + width, :]
        values = v_ref[begin : begin + width, :]
        pair = []
        for head in range(2):
            mine = low_half if head == 0 else jnp.logical_not(low_half)
            q_head = jnp.where(mine, q_blk, jnp.zeros_like(q_blk))
            scores = dot_last(q_head, keys) * score_scale
            last = jnp.where(tri, scores[:, width - BLK :], -1e30)
            if width > BLK:
                scores = jnp.concatenate([scores[:, : width - BLK], last], axis=1)
            else:
                scores = last
            expo = jnp.exp(scores - jnp.max(scores, axis=1, keepdims=True))
            inverse = 1.0 / jnp.sum(expo, axis=1, keepdims=True)
            probs = (expo * inverse).astype(jnp.bfloat16)
            prob_ref[head, :, offset : offset + width] = probs
            pair.append(jnp.dot(probs, values, preferred_element_type=jnp.float32))
        out_ref[first : first + BLK, :] = jnp.where(low_half, pair[0], pair[1]).astype(jnp.bfloat16)


def attend_fast(mixed):
    rows = mixed.shape[0]
    _, total = row_ranges(rows)
    pairs = HEADS // 2
    return pl.pallas_call(
        lambda *refs: attend_kernel(rows, *refs),
        grid=(pairs,),
        in_specs=[
            pl.BlockSpec((rows, 2 * HD), lambda j: (0, j)),
            pl.BlockSpec((rows, 2 * HD), lambda j: (0, j + HEADS // 2)),
            pl.BlockSpec((rows, 2 * HD), lambda j: (0, j + HEADS)),
        ],
        out_specs=[
            pl.BlockSpec((rows, 2 * HD), lambda j: (0, j)),
            pl.BlockSpec((2, BLK, total), lambda j: (j, 0, 0)),
        ],
        out_shape=[
            jax.ShapeDtypeStruct((rows, D), jnp.bfloat16),
            jax.ShapeDtypeStruct((HEADS, BLK, total), jnp.bfloat16),
        ],
        cost_estimate=pl.CostEstimate(
            flops=8 * HEADS * HD * BLK * total, bytes_accessed=6_000_000, transcendentals=HEADS * BLK * total
        ),
    )(mixed, mixed, mixed)


def attend_back_kernel(rows, q_ref, k_ref, v_ref, prob_ref, dh_ref, out_ref, dk_ref, dv_ref):
    pair_id = pl.program_id(0)
    low_half = lax.broadcasted_iota(jnp.int32, (BLK, 2 * HD), 1) < HD
    dk_ref[...] = jnp.zeros_like(dk_ref)
    dv_ref[...] = jnp.zeros_like(dv_ref)
    ranges, _ = row_ranges(rows)
    column = pl.multiple_of(pair_id * (2 * HD), 2 * HD)
    for first, begin, width, offset in ranges:
        q_blk = q_ref[first : first + BLK, :]
        dh_blk = dh_ref[first : first + BLK, :]
        keys = k_ref[begin : begin + width, :]
        values = v_ref[begin : begin + width, :]
        d_query = []
        for head in range(2):
            mine = low_half if head == 0 else jnp.logical_not(low_half)
            dh_head = jnp.where(mine, dh_blk, jnp.zeros_like(dh_blk))
            q_head = jnp.where(mine, q_blk, jnp.zeros_like(q_blk))
            probs = prob_ref[head, :, offset : offset + width]
            prob_rows = probs.astype(jnp.float32)
            d_prob = dot_last(dh_head, values)
            centre = jnp.sum(prob_rows * d_prob, axis=1, keepdims=True)
            d_scores = (prob_rows * (d_prob - centre)).astype(jnp.bfloat16)
            d_query.append(jnp.dot(d_scores, keys, preferred_element_type=jnp.float32))
            dk_ref[begin : begin + width, :] += dot_first(d_scores, q_head)
            dv_ref[begin : begin + width, :] += dot_first(probs, dh_head)
        joined = score_scale * jnp.where(low_half, d_query[0], d_query[1])
        out_ref[first : first + BLK, pl.ds(column, 2 * HD)] = joined.astype(jnp.bfloat16)
    out_ref[:, pl.ds(column + D, 2 * HD)] = (score_scale * dk_ref[...]).astype(jnp.bfloat16)
    out_ref[:, pl.ds(column + 2 * D, 2 * HD)] = dv_ref[...].astype(jnp.bfloat16)


def attend_back_fast(mixed, probs, d_heads):
    rows = mixed.shape[0]
    _, total = row_ranges(rows)
    return pl.pallas_call(
        lambda *refs: attend_back_kernel(rows, *refs),
        grid=(HEADS // 2,),
        in_specs=[
            pl.BlockSpec((rows, 2 * HD), lambda j: (0, j)),
            pl.BlockSpec((rows, 2 * HD), lambda j: (0, j + HEADS // 2)),
            pl.BlockSpec((rows, 2 * HD), lambda j: (0, j + HEADS)),
            pl.BlockSpec((2, BLK, total), lambda j: (j, 0, 0)),
            pl.BlockSpec((rows, 2 * HD), lambda j: (0, j)),
        ],
        out_specs=pl.BlockSpec((rows, 3 * D), lambda j: (0, 0)),
        out_shape=jax.ShapeDtypeStruct((rows, 3 * D), jnp.bfloat16),
        scratch_shapes=[pltpu.VMEM((rows, 2 * HD), jnp.float32)] * 2,
        cost_estimate=pl.CostEstimate(
            flops=16 * HEADS * HD * BLK * total, bytes_accessed=9_000_000, transcendentals=0
        ),
    )(mixed, mixed, mixed, probs, d_heads)


def bits_of(index, count):
    return [(index // (2**b)) % 2 for b in range(count)]


def partner(values, axis, bit, size):
    return lax.ppermute(values, axis, [(i, i ^ (1 << bit)) for i in range(size)])


def pick(values, which, dim):
    return lax.dynamic_slice_in_dim(values, which, 1, dim)


def scatter_sum(grads, steps, sizes, position):
    for number, (axis, bit, dim) in enumerate(steps):
        here = position[axis][bit]
        recv = partner(pick(grads, 1 - here, dim), axis, bit, sizes[axis])
        kept = pick(grads, here, dim)
        total = kept.astype(jnp.float32) + recv.astype(jnp.float32)
        grads = total if number == len(steps) - 1 else total.astype(grads.dtype)
    return grads


def fast_local(
    sizes,
    inputs,
    order,
    lengths,
    cotangent,
    weight_qkv,
    bias_qv,
    weight_out,
    bias_out,
    weight_in,
    bias_in,
    weight_back,
    bias_back,
    gain_first,
    shift_first,
    gain_second,
    shift_second,
):
    me = lax.axis_index("seq")
    half = inputs.shape[2]
    rows = 2 * half
    n_bits = sizes["fsdp"].bit_length() - 1
    shards = sizes["seq"] * sizes["fsdp"]
    position = {"seq": [me], "fsdp": bits_of(lax.axis_index("fsdp"), n_bits)}
    vectors = (
        bias_qv,
        bias_out,
        bias_in,
        bias_back,
        gain_first,
        shift_first,
        gain_second,
        shift_second,
    )
    part = weight_qkv.shape[0]

    both = jnp.stack([inputs[:, 0], cotangent[:, 0]], axis=1)
    kept = pick(both, me, 0)[0]
    recv = partner(pick(both, 1 - me, 0)[0], "seq", 0, 2)
    slots = lax.dynamic_slice_in_dim(order[:, 0], me, 1, 0)[0].reshape(2, half)
    slots = jnp.concatenate([pick(slots, me, 0)[0], pick(slots, 1 - me, 0)[0]])
    first_len = lax.dynamic_slice_in_dim(lengths[:, 0, 0], me, 1, 0)[0]
    moved = jnp.where(slots >= first_len, slots - first_len, slots + (rows - first_len))
    place = jnp.where(first_len == rows * 3 // 4, slots, moved)
    select = (place[None, :] == jnp.arange(rows, dtype=place.dtype)[:, None]).astype(jnp.bfloat16)
    x_rows = jnp.dot(select, jnp.concatenate([kept[0], recv[0]]), preferred_element_type=jnp.bfloat16)
    grad_rows = jnp.dot(
        select, jnp.concatenate([kept[1], recv[1]]), preferred_element_type=jnp.bfloat16
    )

    flat = jnp.concatenate(vectors)
    flat = jnp.pad(flat, (0, 8 * D - flat.shape[0])).reshape(8, D)
    pieces = [weight_qkv[:, i * D : (i + 1) * D] for i in range(3)]
    pieces += [weight_in[:, i * D : (i + 1) * D] for i in range(weight_in.shape[1] // D)]
    pieces += [weight_out, weight_back, flat]
    packed = jnp.concatenate(pieces)
    whole = lax.all_gather(packed, ("seq", "fsdp"), axis=0, tiled=True).reshape(shards, -1, D)
    mats = [whole[:, i * part : (i + 1) * part].reshape(D, D) for i in range(8)]
    qkv_mat = jnp.concatenate(mats[:3], axis=1)
    in_mat = jnp.concatenate(mats[3:7], axis=1)
    out_mat = mats[7]
    after = 8 * part
    back_rows = weight_back.shape[0]
    back_mat = whole[:, after : after + back_rows].reshape(back_rows * shards, D)
    vec_rows = whole[:, after + back_rows :].reshape(shards, 8 * D)
    gathered, start = [], 0
    for vec in vectors:
        width = vec.shape[0]
        gathered.append(vec_rows[:, start : start + width].reshape(-1))
        start += width
    qv_vec, out_vec, in_vec, back_vec, gain_one, shift_one, gain_two, shift_two = gathered

    x_float = x_rows.astype(jnp.float32)
    x_hat_one, inv_one = norm_parts(x_float)
    normed = (x_hat_one * gain_one + shift_one).astype(jnp.bfloat16)
    projected = jnp.dot(normed, qkv_mat, preferred_element_type=jnp.float32)
    qkv_vec = jnp.concatenate([qv_vec[:D], jnp.zeros((D,), qv_vec.dtype), qv_vec[D:]])
    mixed = (projected + qkv_vec).astype(jnp.bfloat16)
    attn_heads, probs = attend_fast(mixed)
    mid_stream = (
        x_float + jnp.dot(attn_heads, out_mat, preferred_element_type=jnp.float32) + out_vec
    )
    x_hat_two, inv_two = norm_parts(mid_stream)
    normed_two = (x_hat_two * gain_two + shift_two).astype(jnp.bfloat16)
    pre_act = jnp.dot(normed_two, in_mat, preferred_element_type=jnp.float32) + in_vec
    hidden_float, gelu_pull = jax.vjp(gelu_tanh, pre_act)
    hidden = hidden_float.astype(jnp.bfloat16)
    result = mid_stream + jnp.dot(hidden, back_mat, preferred_element_type=jnp.float32) + back_vec
    result = result.astype(jnp.bfloat16)

    low, high = ("fsdp", 0, n_bits), ("fsdp", 1, n_bits - 1)
    rest = [("fsdp", b, n_bits - b) for b in range(2, n_bits)]
    order_a = [("seq", 0, 0), low, high] + rest
    order_b = [("seq", 0, 0), high, low] + rest
    cube = (2,) * (n_bits + 1)

    def reduce_rows(grad, steps):
        grad = grad.astype(jnp.bfloat16)
        shard_rows = grad.shape[0] // shards
        total = scatter_sum(
            grad.reshape(cube + (shard_rows, grad.shape[1])), steps, sizes, position
        )
        return total.reshape(shard_rows, grad.shape[1])

    grad_float = grad_rows.astype(jnp.float32)
    d_back_mat = reduce_rows(dot_first(hidden, grad_rows), order_a)
    d_back_vec = jnp.sum(grad_float, axis=0)
    d_hidden = dot_last(grad_rows, back_mat)
    d_pre = gelu_pull(d_hidden)[0].astype(jnp.bfloat16)
    d_in_mat = reduce_rows(dot_first(normed_two, d_pre), order_b)
    d_in_vec = jnp.sum(d_pre.astype(jnp.float32), axis=0)
    d_norm_two = dot_last(d_pre, in_mat)
    d_gain_two = jnp.sum(d_norm_two * x_hat_two, axis=0)
    d_shift_two = jnp.sum(d_norm_two, axis=0)
    d_mid = grad_float + norm_back(d_norm_two, x_hat_two, inv_two, gain_two)
    d_out_vec = jnp.sum(d_mid, axis=0)
    d_mid_low = d_mid.astype(jnp.bfloat16)
    d_out_mat = reduce_rows(dot_first(attn_heads, d_mid_low), order_a)
    d_heads = dot_last(d_mid_low, out_mat).astype(jnp.bfloat16)
    d_mixed = attend_back_fast(mixed, probs, d_heads)
    cut = 3 * D // 2
    d_qkv_mat = jnp.concatenate(
        [
            reduce_rows(dot_first(normed, d_mixed[:, :cut]), order_a),
            reduce_rows(dot_first(normed, d_mixed[:, cut:]), order_b),
        ],
        axis=1,
    )
    column_sums = jnp.sum(d_mixed.astype(jnp.float32), axis=0)
    d_qv_vec = jnp.concatenate([column_sums[:D], column_sums[2 * D :]], axis=0)
    d_norm_one = dot_last(d_mixed, qkv_mat)
    d_gain_one = jnp.sum(d_norm_one * x_hat_one, axis=0)
    d_shift_one = jnp.sum(d_norm_one, axis=0)
    d_inputs = d_mid + norm_back(d_norm_one, x_hat_one, inv_one, gain_one)
    d_inputs = d_inputs.astype(jnp.bfloat16)

    small = (
        d_qv_vec,
        d_out_vec,
        d_in_vec,
        d_back_vec,
        d_gain_one,
        d_shift_one,
        d_gain_two,
        d_shift_two,
    )
    joined = jnp.concatenate([v.reshape(shards, -1) for v in small], axis=1)
    joined = scatter_sum(joined.reshape(cube + (1, -1)), order_a, sizes, position).reshape(-1)
    small_out, start = [], 0
    for vec in vectors:
        small_out.append(joined[start : start + vec.shape[0]])
        start += vec.shape[0]

    def give_back(sorted_rows):
        slot_rows = lax.dot_general(
            select, sorted_rows, (((0,), (0,)), ((), ())), preferred_element_type=jnp.bfloat16
        )
        other = partner(slot_rows[half:], "seq", 0, 2)
        own = slot_rows[:half]
        first = jnp.where(me == 0, own, other)
        second = jnp.where(me == 0, other, own)
        return jnp.stack([first, second])[:, None]

    return (
        give_back(result),
        give_back(d_inputs),
        d_qkv_mat,
        small_out[0],
        d_out_mat,
        small_out[1],
        d_in_mat,
        small_out[2],
        d_back_mat,
        small_out[3],
        small_out[4],
        small_out[5],
        small_out[6],
        small_out[7],
    )


def takes_fast(mesh):
    fsdp = mesh.shape["fsdp"]
    return mesh.shape["seq"] == MB == 2 and fsdp >= 4 and fsdp & (fsdp - 1) == 0


def solution(mesh):
    if takes_fast(mesh):
        sizes = dict(mesh.shape)
        body = lambda *arrays: fast_local(sizes, *arrays)
    else:
        body = local
    return jax.shard_map(
        body,
        mesh=mesh,
        in_specs=(
            P(None, "fsdp", "seq", None),
            P(None, "fsdp", None),
            P(None, "fsdp", None),
            P(None, "fsdp", "seq", None),
            P(("seq", "fsdp"), None),
            P(("seq", "fsdp")),
            P(("seq", "fsdp"), None),
            P(("seq", "fsdp")),
            P(("seq", "fsdp"), None),
            P(("seq", "fsdp")),
            P(("seq", "fsdp"), None),
            P(("seq", "fsdp")),
            P(("seq", "fsdp")),
            P(("seq", "fsdp")),
            P(("seq", "fsdp")),
            P(("seq", "fsdp")),
        ),
        out_specs=(
            P(None, "fsdp", "seq", None),
            P(None, "fsdp", "seq", None),
            P(("seq", "fsdp"), None),
            P(("seq", "fsdp")),
            P(("seq", "fsdp"), None),
            P(("seq", "fsdp")),
            P(("seq", "fsdp"), None),
            P(("seq", "fsdp")),
            P(("seq", "fsdp"), None),
            P(("seq", "fsdp")),
            P(("seq", "fsdp")),
            P(("seq", "fsdp")),
            P(("seq", "fsdp")),
            P(("seq", "fsdp")),
        ),
        check_vma=False,
    )
```
